256 devices in a mesh: dp: 16 (over y, x_hi, core), tensor: 16 (over z, x_lo).
Axes of the slice: x: 4 (x_hi: 2, x_lo: 2; x = x_hi * 2 + x_lo), y: 4, z: 8, core: 2. Of those that a mesh axis runs over, the one named last changes fastest.
Arguments:
- acts: bfloat16 [2048, 4096], P(('dp', 'tensor')), may hold values from -6 to 6
- gate_pre: bfloat16 [2048, 14336], P('dp', 'tensor'), may hold values from -8 to 8
- up_pre: bfloat16 [2048, 14336], P('dp', 'tensor'), may hold values from -6 to 6
- out_grad: bfloat16 [2048, 4096], P(('dp', 'tensor')), may hold values from -24 to 24
- segments: int32 [16, 128], P('dp', 'tensor'), may hold values from 0 to 23, never falling along the last dimension, each value on 1 to 32 neighbouring positions
- down_weight: bfloat16 [4096, 14336], P(None, 'tensor'), may hold values from -0.046875 to 0.046875
Outputs:
- grad_gate: float32 [4096, 14336], P('dp', 'tensor')
- grad_up: float32 [4096, 14336], P('dp', 'tensor')
- grad_down: float32 [4096, 14336], P('dp', 'tensor')
The draws below stay inside these ranges and needn't reach their ends.
Inputs may be any that keep to these rules, and one draw needn't show every extreme that they name: `segments`: within each group ids never fall; each id that occurs covers 1 to 32 tokens, and some id covers exactly that many.
All inputs are finite; a program needn't handle non-finite values.
Results may differ from the reference program's by a relative error of at most 0.014.
Values may be sent and summed in bfloat16 or wider, within the bound.
No kernel may reach another device: no remote copies, remote signals or barrier semaphores. Data moves between devices by JAX's collectives and lax.ppermute only.
A program may use at most 128 MiB of HBM per device.

```python
import math
import jax
import jax.numpy as jnp
import numpy as np
from jax import lax

D = 4096
FF = 14336
SEGS = 24
TOK_GROUP = 128
TOKENS = 2048
N_DP = 16


def with_spikes(result, rng, source, target, blocks, factor):
    owner, partner = [(jnp.arange(result.shape[axis_at]) // (result.shape[axis_at] // blocks)).reshape([-1 if axis == axis_at else 1 for axis in range(result.ndim)]) for axis_at in (source, target)]
    chosen = jax.random.permutation(rng, blocks)[partner]
    strong = (owner == chosen) | (owner == (partner + blocks // 2) % blocks)
    return jnp.where(strong, factor * result, result)


def block_scale(key, extent, pieces, smallest, top_value):
    def one(axis_at, shards_of):
        heights = jax.random.uniform(jax.random.fold_in(jax.random.fold_in(key, 6), axis_at), (shards_of,), jnp.float32, smallest / len(pieces), top_value / len(pieces))
        return jnp.repeat(jnp.exp(heights), extent[axis_at] // shards_of).reshape((-1,) + (1,) * (len(extent) - axis_at - 1))

    gain = one(*pieces[0])
    for cut in pieces[1:]:
        gain = gain * one(*cut)
    return gain


def length_profile(count, total, reach, slope):
    loads = [(1 << 20) // math.isqrt(standing ** slope) + 1 for standing in range(2, count + 1)]
    rest, given = total - reach - (count - 1), [1] * (count - 1)
    while rest > 0:
        movable = [i for i in range(count - 1) if given[i] < reach]
        mass, left = sum([loads[i] for i in movable]), rest
        for i in movable:
            more = min(reach - given[i], max(1, left * loads[i] // mass), rest)
            given[i] = given[i] + more
            rest = rest - more
    return np.array([reach] + given)


def ragged_sizes(key, number_of, total, bound, lean):
    if number_of == 2:
        one = jax.random.randint(key, (), max(1, total - bound), min(bound, total - 1) + 1)
        return jnp.stack([one, total - one])
    lengths = jnp.asarray(length_profile(number_of, total, bound, lean), jnp.int32)
    twos = (number_of - 1) // 2
    source_of, sink = lengths[1:1 + 2 * twos:2], lengths[2:2 + 2 * twos:2]
    margin = jnp.minimum(source_of - 1, bound - sink)
    passed = jax.random.randint(jax.random.fold_in(key, 1), (twos,), 0, 1 << 20) % (margin + 1)
    lengths = lengths.at[1:1 + 2 * twos:2].set(source_of - passed).at[2:2 + 2 * twos:2].set(sink + passed)
    return lengths[jax.random.permutation(jax.random.fold_in(key, 2), number_of)]


def bell_draw(rng, shape, deviation, most, shards=(), kind=jnp.bfloat16):
    gain = block_scale(rng, shape, shards, -0.22, 0.18) if shards else 1.0
    values = jax.random.normal(rng, shape, jnp.float32) * deviation * gain
    return jnp.minimum(jnp.maximum(values, -most), most).astype(kind)


def bell_draw_with(key, shape, scale, most, pieces, heavy, held_as=jnp.bfloat16):
    drawn = scale * jax.random.normal(key, shape, jnp.float32)
    if pieces:
        drawn = drawn * block_scale(key, shape, pieces, -0.22, 0.18)
    return jnp.clip(with_spikes(drawn, jax.random.fold_in(key, 3), *heavy), -most, most).astype(held_as)


def setup_inputs(seed: int = 0) -> dict:
    streams_of = jax.random.split(jax.random.key(seed), 7)
    acts = bell_draw(streams_of[0], (TOKENS, D), 1.0, 6.0, ((0, 256),))
    gate_pre = bell_draw(streams_of[1], (TOKENS, FF), 1.5, 8.0, ((0, 16), (1, 16)))
    up_pre = bell_draw(streams_of[2], (TOKENS, FF), 1.0, 6.0, ((0, 16), (1, 16)))
    out_grad = bell_draw_with(streams_of[3], (TOKENS, D), 1.0, 24.0, ((0, 256),), (0, 1, 256, 6.0))
    segments = jax.vmap(lambda own: jnp.searchsorted(jnp.cumsum(ragged_sizes(own, SEGS, TOK_GROUP, TOK_GROUP // 4, 1)), jnp.arange(TOK_GROUP), side="right"))(jax.random.split(streams_of[4], N_DP)).reshape((N_DP, TOK_GROUP)).astype(jnp.int32)
    down_weight = bell_draw(streams_of[5], (D, FF), FF ** -0.5, 0.046875, ((1, 16),))
    return dict(acts=acts, gate_pre=gate_pre, up_pre=up_pre, out_grad=out_grad, segments=segments, down_weight=down_weight)


def token_weights(seg_ids):
    table = jnp.arange(SEGS, dtype=jnp.int32)
    onehot = (seg_ids[:, None] == table[None, :]).astype(jnp.float32)
    counts = jnp.sum(onehot, axis=0)
    own = jnp.sum(onehot * counts[None, :], axis=1)
    return 1.0 / own


def rounded(value):
    return lax.optimization_barrier(value.astype(jnp.bfloat16)).astype(jnp.float32)


def reference(acts, gate_pre, up_pre, out_grad, segments, down_weight):
    inputs = acts.reshape(N_DP, TOK_GROUP, D)
    grads = out_grad.reshape(N_DP, TOK_GROUP, D)
    gates = gate_pre.reshape(N_DP, TOK_GROUP, FF)
    ups = up_pre.reshape(N_DP, TOK_GROUP, FF)

    def one_group(carry, item):
        x_rows, dy_rows, g_rows, u_rows, seg_rows = item
        weights = token_weights(seg_rows)
        gate = g_rows.astype(jnp.float32)
        up = u_rows.astype(jnp.float32)
        sigma = jax.nn.sigmoid(gate)
        active = gate * sigma
        hidden_grad = weights[:, None] * jnp.dot(dy_rows, down_weight, preferred_element_type=jnp.float32)
        gate_grad = (hidden_grad * up * sigma * (1.0 + gate * (1.0 - sigma))).astype(jnp.bfloat16)
        up_grad = (hidden_grad * active).astype(jnp.bfloat16)
        weighted_hidden = (weights[:, None] * active * up).astype(jnp.bfloat16)
        part_gate = rounded(jnp.dot(x_rows.T, gate_grad, preferred_element_type=jnp.float32))
        part_up = rounded(jnp.dot(x_rows.T, up_grad, preferred_element_type=jnp.float32))
        part_down = rounded(jnp.dot(dy_rows.T, weighted_hidden, preferred_element_type=jnp.float32))
        return (carry[0] + part_gate, carry[1] + part_up, carry[2] + part_down), None

    zeros = jnp.zeros((D, FF), jnp.float32)
    totals, unused = lax.scan(one_group, (zeros, zeros, zeros), (inputs, grads, gates, ups, segments))
    return (totals[0], totals[1], totals[2])
```

```python
import jax
import jax.numpy as jnp
from jax import lax
from jax.experimental import pallas as pl
from jax.experimental.pallas import tpu as pltpu
from jax.sharding import PartitionSpec as P

BF = jnp.bfloat16
F32 = jnp.float32
VMEM = pl.BlockSpec(memory_space=pltpu.VMEM)

PIECES = [(ky, kx) for ky in range(4) for kx in range(2)]
Z_STEPS = [0, 1, 2, 3, 4, -1, -2, -3]


def over_dp(ky, kx):
    return [
        (d, ((d // 4 + ky) % 4) * 4 + (((d // 2) % 2) ^ kx) * 2 + d % 2) for d in range(16)
    ]


def over_z(step):
    return [(t, ((t // 2 + step) % 8) * 2 + t % 2) for t in range(16)]


OVER_CORE = [(d, d ^ 1) for d in range(16)]
OVER_XL = [(t, t ^ 1) for t in range(16)]


def send_dp(value, ky, kx):
    return lax.ppermute(value, "dp", over_dp(ky, kx))


def send_z(value, step):
    return lax.ppermute(value, "tensor", over_z(step))


def call(kernel, outs, args, name, flops=0, scratch=(), limit=None):
    moved = sum(a.size * a.dtype.itemsize for a in list(args) + list(outs))
    return pl.pallas_call(
        kernel,
        out_shape=outs,
        in_specs=[VMEM] * len(args),
        out_specs=[VMEM] * len(outs),
        scratch_shapes=scratch,
        name=name,
        cost_estimate=pl.CostEstimate(flops=flops, bytes_accessed=moved, transcendentals=0),
        compiler_params=pltpu.CompilerParams(vmem_limit_bytes=limit) if limit else None,
    )(*args)


def sds(shape, dtype=BF):
    return jax.ShapeDtypeStruct(shape, dtype)


def stack_two(a_ref, b_ref, out_ref):
    out_ref[0] = a_ref[...]
    out_ref[1] = b_ref[...]


def pack(x_ref, xo_ref, dy_ref, dyo_ref, seg_ref, sego_ref, both_ref, *msgs):
    d = lax.axis_index("dp")
    y, xh, core = d // 4, (d // 2) % 2, d % 2
    both_ref[0] = dy_ref[...]
    both_ref[1] = dyo_ref[...]
    for (ky, kx), msg in zip(PIECES, msgs):
        block = ((y + ky) % 4) * 2 + jnp.where(xh == kx, 0, 1)
        for half in range(2):
            own = core if half == 0 else 1 - core
            cols = pl.ds(pl.multiple_of(block * 512 + own * 256, 256), 256)
            for e, (x, dy, seg) in enumerate(
                ((x_ref, dy_ref, seg_ref), (xo_ref, dyo_ref, sego_ref))
            ):
                msg[e, :, half * 256 : half * 256 + 256] = x[:, cols]
                msg[e, :, 512 + half * 256 : 768 + half * 256] = dy[:, cols]
                if half == 0:
                    msg[e, :, 1024:1152] = seg[...]


def stack_pieces(*refs):
    for k in range(8):
        refs[8][k] = refs[k][...]


def source_row(step, e):
    t = lax.axis_index("tensor")
    z, xl = t // 2, t % 2
    return ((z - step + 8) % 8) * 2 + (xl if e == 0 else 1 - xl)


def hidden(*refs):
    pieces, w_ref, out_ref, lhs = refs[:8], refs[8], refs[9], refs[10]
    for i in range(8):
        lhs[16 * i : 16 * i + 16, :] = pieces[i][...].reshape(16, 4096)
    acc = jnp.dot(lhs[...], w_ref[...], preferred_element_type=F32)
    for i, step in enumerate(Z_STEPS):
        for e in range(2):
            row = 16 * i + 8 * e
            out_ref[source_row(step, e)] = acc[row : row + 8, :].astype(BF)


def factors(*refs):
    pieces, (a1_ref, a2_ref, a3_ref) = refs[:-3], refs[-3:]
    for k in range(len(pieces)):

        @pl.loop(0, 8)
        def _(r):
            rows = pl.ds(pl.multiple_of(r * 16, 16), 16)
            gate = pieces[k][0, rows, :].astype(F32)
            up = pieces[k][1, rows, :].astype(F32)
            sigma = jax.nn.sigmoid(gate)
            active = gate * sigma
            a1_ref[k, rows, :] = (up * sigma * (1.0 + gate * (1.0 - sigma))).astype(BF)
            a2_ref[k, rows, :] = active.astype(BF)
            a3_ref[k, rows, :] = (active * up).astype(BF)


def assemble(*refs):
    pieces, xw_ref, dyw_ref, raw, seg = refs[:8], refs[8], refs[9], refs[10], refs[11]
    for i, step in enumerate(Z_STEPS):
        for e in range(2):
            t = source_row(step, e)
            for k in range(8):
                raw[k, t] = pieces[i][k, e, :, :1024].astype(F32)
                seg[k, t] = pieces[i][k, e, :, 1024:].astype(F32)
    for k in range(8):
        ids = seg[k].reshape(128, 128)
        count = jnp.sum((ids == ids.T).astype(F32), axis=1, keepdims=True)
        weighted = raw[k].reshape(128, 1024) * (1.0 / count)
        xw_ref[128 * k : 128 * k + 128, :] = weighted[:, :512].astype(BF)
        dyw_ref[128 * k : 128 * k + 128, :] = weighted[:, 512:].astype(BF)


def contract(left, right):
    return lax.dot_general(left, right, (((0,), (0,)), ((), ())), preferred_element_type=F32)


def partial_down(dyw_ref, a3_ref, own_ref, other_ref):
    right = a3_ref[...].reshape(1024, 896)
    own_ref[...] = contract(dyw_ref[:, :256], right)
    other_ref[...] = contract(dyw_ref[:, 256:], right).astype(BF)


def partial_in(*refs):
    xw_ref, a_ref, pieces, own_ref, other_ref, grad = (
        refs[0],
        refs[1],
        refs[2:10],
        refs[10],
        refs[11],
        refs[12],
    )
    for k in range(8):
        h = pieces[k][...].reshape(128, 896).astype(F32)
        grad[128 * k : 128 * k + 128, :] = (h * a_ref[k].astype(F32)).astype(BF)
    own_ref[...] = contract(xw_ref[:, :256], grad[...])
    other_ref[...] = contract(xw_ref[:, 256:], grad[...]).astype(BF)


def gather_groups(value):
    across = send_dp(value, 0, 1)
    up, down = send_dp(value, 1, 0), send_dp(value, 3, 0)
    up_across, down_across = send_dp(across, 1, 0), send_dp(across, 3, 0)
    far = send_dp(up, 1, 0)
    far_across = send_dp(down_across, 3, 0)
    return [value, across, up, up_across, far, far_across, down, down_across]


def body(acts, gate_pre, up_pre, out_grad, segments, down_weight):
    seg = jnp.broadcast_to(segments.reshape(8, 1).astype(BF), (8, 128))
    out_grad_o = lax.ppermute(out_grad, "tensor", OVER_XL)
    acts_o = lax.ppermute(acts, "tensor", OVER_XL)
    seg_o = lax.ppermute(seg, "tensor", OVER_XL)
    (pair,) = call(stack_two, [sds((2, 128, 896))], (gate_pre, up_pre), "pair")

    packed = call(
        pack,
        [sds((2, 8, 4096))] + [sds((2, 8, 1152))] * 8,
        (acts, acts_o, out_grad, out_grad_o, seg, seg_o),
        "pack",
    )
    both, msgs = packed[0], packed[1:]
    grads = [both] + [send_z(both, s) for s in Z_STEPS[1:]]
    (hid,) = call(
        hidden,
        [sds((16, 8, 896))],
        (*grads, down_weight),
        "hidden",
        flops=2 * 128 * 4096 * 896,
        scratch=[pltpu.VMEM((128, 4096), BF)],
    )

    cols = [msgs[0]] + [send_dp(m, *k) for m, k in zip(msgs[1:], PIECES[1:])]
    (block,) = call(stack_pieces, [sds((8, 2, 8, 1152))], cols, "columns")
    ahead, back = [block], [block]
    for _ in range(4):
        ahead.append(send_z(ahead[-1], 1))
    for _ in range(3):
        back.append(send_z(back[-1], -1))
    xw, dyw = call(
        assemble,
        [sds((1024, 512))] * 2,
        ahead + back[1:],
        "assemble",
        flops=20 * 1024 * 1024,
        scratch=[pltpu.VMEM((8, 16, 8, 1024), F32), pltpu.VMEM((8, 16, 8, 128), F32)],
    )

    pairs = gather_groups(pair)
    a1, a2, a3 = call(
        factors, [sds((8, 128, 896))] * 3, pairs, "factors", flops=30 * 1024 * 896
    )
    down_own, down_other = call(
        partial_down,
        [sds((256, 896), F32), sds((256, 896))],
        (dyw, a3),
        "down",
        flops=2 * 1024 * 512 * 896,
    )
    down_in = lax.ppermute(down_other, "dp", OVER_CORE)

    hids = gather_groups(hid)
    results = []
    for a, name in ((a1, "gate"), (a2, "up")):
        own, other = call(
            partial_in,
            [sds((256, 896), F32), sds((256, 896))],
            (xw, a, *hids),
            name,
            flops=2 * 1024 * 512 * 896,
            scratch=[pltpu.VMEM((1024, 896), BF)],
        )
        results.append(own + lax.ppermute(other, "dp", OVER_CORE).astype(F32))
    return results[0], results[1], down_own + down_in.astype(F32)


def solution(mesh):
    in_specs = (
        P(("dp", "tensor"), None),
        P("dp", "tensor"),
        P("dp", "tensor"),
        P(("dp", "tensor"), None),
        P("dp", "tensor"),
        P(None, "tensor"),
    )
    out_specs = (P("dp", "tensor"), P("dp", "tensor"), P("dp", "tensor"))
    return jax.shard_map(body, mesh=mesh, in_specs=in_specs, out_specs=out_specs, check_vma=False)
```

```python
import jax
import jax.numpy as jnp
from jax import lax
from jax.experimental import pallas as pl
from jax.experimental.pallas import tpu as pltpu
from jax.sharding import PartitionSpec as P


BF = jnp.bfloat16
F32 = jnp.float32
VMEM = pl.BlockSpec(memory_space=pltpu.VMEM)
HBM = pl.BlockSpec(memory_space=pltpu.HBM)

PIECES = [(ky, kx) for ky in range(4) for kx in range(2)]
Z_STEPS = [0, 1, 2, 3, 4, -1, -2, -3]
GRAD_STEPS = [0, 1, -1, 2, -2, 3, -3, 4]


def over_dp(ky, kx):
    return [
        (d, ((d // 4 + ky) % 4) * 4 + (((d // 2) % 2) ^ kx) * 2 + d % 2) for d in range(16)
    ]


def over_z(step):
    return [(t, ((t // 2 + step) % 8) * 2 + t % 2) for t in range(16)]


OVER_CORE = [(d, d ^ 1) for d in range(16)]
OVER_XL = [(t, t ^ 1) for t in range(16)]


def send_dp(value, ky, kx):
    return lax.ppermute(value, "dp", over_dp(ky, kx))


def send_z(value, step):
    return lax.ppermute(value, "tensor", over_z(step))


def send_core(value):
    return lax.ppermute(value, "dp", OVER_CORE)


def send_xl(value):
    return lax.ppermute(value, "tensor", OVER_XL)


def call(kernel, outs, args, flops=0, scratch=(), spec=VMEM):
    if spec is HBM:
        args = [pltpu.with_memory_space_constraint(a, pltpu.HBM) for a in args]
    moved = sum(a.size * a.dtype.itemsize for a in list(args) + list(outs))
    return pl.pallas_call(
        kernel,
        out_shape=outs,
        in_specs=[spec] * len(args),
        out_specs=[VMEM] * len(outs),
        scratch_shapes=scratch,
        cost_estimate=pl.CostEstimate(flops=flops, bytes_accessed=moved, transcendentals=0),
        compiler_params=pltpu.CompilerParams(vmem_limit_bytes=20 * 2**20),
    )(*args)


def sds(shape, dtype=BF):
    return jax.ShapeDtypeStruct(shape, dtype)


def stack_two(a_ref, b_ref, out_ref):
    out_ref[0] = a_ref[...]
    out_ref[1] = b_ref[...]


def load(
    x_ref, seg_ref, dy_ref, gate_ref, up_ref, rows_ref, dy_out_ref, pair_ref, ids_ref, sems
):
    copies = [
        pltpu.make_async_copy(src, dst, sems.at[i])
        for i, (src, dst) in enumerate(
            (
                (seg_ref, ids_ref),
                (x_ref, rows_ref.at[:, pl.ds(0, 4096)]),
                (dy_ref, dy_out_ref),
                (gate_ref, pair_ref.at[0]),
                (up_ref, pair_ref.at[1]),
            )
        )
    ]
    for copy in copies:
        copy.start()
    copies[0].wait()
    rows = lax.broadcasted_iota(jnp.int32, (8, 8), 0)
    cols = lax.broadcasted_iota(jnp.int32, (8, 8), 1)
    ids = jnp.broadcast_to(ids_ref[...].astype(F32), (8, 8))
    ids = jnp.sum(jnp.where(rows == cols, ids, 0.0), axis=1, keepdims=True)
    rows_ref[:, 4096:] = jnp.broadcast_to(ids, (8, 128)).astype(BF)
    for copy in copies[1:]:
        copy.wait()


def fetch(src_ref, dst_ref, sems):
    copies = [
        pltpu.make_async_copy(
            src_ref.at[pl.ds(i * 512, 512)], dst_ref.at[pl.ds(i * 512, 512)], sems.at[i]
        )
        for i in range(8)
    ]
    for copy in copies:
        copy.start()
    for copy in copies:
        copy.wait()


def pack(x_ref, xo_ref, dy_ref, dyo_ref, near_ref, across_ref):
    d = lax.axis_index("dp")
    y, xh, core = d // 4, (d // 2) % 2, d % 2
    for ky, kx in PIECES:
        msg = (across_ref if kx else near_ref).at[ky]
        block = ((y + ky) % 4) * 2 + jnp.where(xh == kx, 0, 1)
        for e, (x, dy) in enumerate(((x_ref, dy_ref), (xo_ref, dyo_ref))):
            for half in range(2):
                own = core if half == 0 else 1 - core
                cols = pl.ds(pl.multiple_of(block * 512 + own * 256, 256), 256)
                msg[e, :, half * 256 : half * 256 + 256] = x[:, cols]
                msg[e, :, 512 + half * 256 : 768 + half * 256] = dy[:, cols]
            msg[e, :, 1024:1152] = x[:, 4096:]


def repack(near_ref, across_ref, *outs):
    for ky in range(4):
        outs[ky][0] = near_ref[ky]
        outs[ky][1] = across_ref[ky]


def stack_pieces(*refs):
    for ky in range(4):
        refs[4][2 * ky : 2 * ky + 2] = refs[ky][...]


def source_row(step, e):
    t = lax.axis_index("tensor")
    z, xl = t // 2, t % 2
    return ((z - step + 8) % 8) * 2 + (xl if e == 0 else 1 - xl)


def hidden(*refs):
    pieces, w_ref, out_ref, lhs = refs[:8], refs[8], refs[9], refs[10]
    for i in range(8):
        lhs[16 * i : 16 * i + 16, :] = pieces[i][...].reshape(16, 4096)
    acc = jnp.dot(lhs[...], w_ref[...], preferred_element_type=F32)
    for i, step in enumerate(GRAD_STEPS):
        for e in range(2):
            row = 16 * i + 8 * e
            out_ref[source_row(step, e)] = acc[row : row + 8, :].astype(BF)


def factors(*refs):
    count = len(refs) // 4
    pieces, outs = refs[:count], refs[count:]
    for k in range(count):

        @pl.loop(0, 8)
        def _(r):
            rows = pl.ds(pl.multiple_of(r * 16, 16), 16)
            gate = pieces[k][0, rows, :].astype(F32)
            up = pieces[k][1, rows, :].astype(F32)
            sigma = jax.nn.sigmoid(gate)
            active = gate * sigma
            slope = up * sigma * (1.0 + gate * (1.0 - sigma))
            for out, value in zip(outs[3 * k : 3 * k + 3], (slope, active, active * up)):
                out[rows, :] = value.astype(BF)


def assemble(*refs):
    pieces, xw_ref, dyw_ref, raw, seg = refs[:8], refs[8], refs[9], refs[10], refs[11]
    for i, step in enumerate(Z_STEPS):
        for e in range(2):
            t = source_row(step, e)
            for k in range(8):
                raw[k, t] = pieces[i][k, e, :, :1024].astype(F32)
                seg[k, t] = pieces[i][k, e, :, 1024:].astype(F32)
    for k in range(8):
        ids = seg[k].reshape(128, 128)
        count = jnp.sum((ids == ids.T).astype(F32), axis=1, keepdims=True)
        weighted = raw[k].reshape(128, 1024) * (1.0 / count)
        xw_ref[128 * k : 128 * k + 128, :] = weighted[:, :512].astype(BF)
        dyw_ref[128 * k : 128 * k + 128, :] = weighted[:, 512:].astype(BF)


def contract(left, right):
    return lax.dot_general(left, right, (((0,), (0,)), ((), ())), preferred_element_type=F32)


def partial_down(*refs):
    dyw_ref, pieces, own_ref, other_ref, right = refs[0], refs[1:9], refs[9], refs[10], refs[11]
    for k in range(8):
        right[128 * k : 128 * k + 128, :] = pieces[k][...]
    own_ref[...] = contract(dyw_ref[:, :256], right[...])
    other_ref[...] = contract(dyw_ref[:, 256:], right[...]).astype(BF)


def partial_in(*refs):
    xw_ref, scales, pieces = refs[0], refs[1:9], refs[9:17]
    own_ref, other_ref, grad = refs[17:]
    for k in range(8):
        h = pieces[k][...].reshape(128, 896).astype(F32)
        grad[128 * k : 128 * k + 128, :] = (h * scales[k][...].astype(F32)).astype(BF)
    own_ref[...] = contract(xw_ref[:, :256], grad[...])
    other_ref[...] = contract(xw_ref[:, 256:], grad[...]).astype(BF)


def gather_groups(value):
    across = send_dp(value, 0, 1)
    up, down = send_dp(value, 1, 0), send_dp(value, 3, 0)
    up_across, down_across = send_dp(across, 1, 0), send_dp(across, 3, 0)
    far = send_dp(up, 1, 0)
    far_across = send_dp(down_across, 3, 0)
    return [value, across, up, up_across, far, far_across, down, down_across]


def body(acts, gate_pre, up_pre, out_grad, segments, down_weight):
    out_grad_o = send_xl(out_grad)
    rows, grad_rows, pair = call(
        load,
        [sds((8, 4224)), sds((8, 4096)), sds((2, 128, 896))],
        (acts, segments, out_grad, gate_pre, up_pre),
        scratch=[pltpu.VMEM((1, 8), jnp.int32), pltpu.SemaphoreType.DMA((5,))],
        spec=HBM,
    )
    rows_o = send_xl(rows)
    pairs = gather_groups(pair)

    (both,) = call(stack_two, [sds((2, 8, 4096))], (grad_rows, out_grad_o))
    near = [send_z(both, 1), send_z(both, -1)]
    far = [send_z(both, 2), send_z(both, -2)]
    farther = [send_z(far[0], 1), send_z(far[1], -1), send_z(far[0], 2)]
    (weight,) = call(
        fetch, [sds((4096, 896))], (down_weight,), scratch=[pltpu.SemaphoreType.DMA((8,))], spec=HBM
    )
    (hid,) = call(
        hidden,
        [sds((16, 8, 896))],
        (both, *near, *far, *farther, weight),
        flops=2 * 128 * 4096 * 896,
        scratch=[pltpu.VMEM((128, 4096), BF)],
    )

    mine, theirs = call(pack, [sds((4, 2, 8, 1152))] * 2, (rows, rows_o, grad_rows, out_grad_o))
    theirs = send_dp(theirs, 0, 1)
    msgs = call(repack, [sds((2, 2, 8, 1152))] * 4, (mine, theirs))
    cols = [msgs[0]] + [send_dp(msgs[ky], ky, 0) for ky in (1, 2, 3)]
    (block,) = call(stack_pieces, [sds((8, 2, 8, 1152))], cols)
    ahead, back = [block], [block]
    for _ in range(4):
        ahead.append(send_z(ahead[-1], 1))
    for _ in range(3):
        back.append(send_z(back[-1], -1))
    xw, dyw = call(
        assemble,
        [sds((1024, 512))] * 2,
        ahead + back[1:],
        flops=20 * 1024 * 1024,
        scratch=[pltpu.VMEM((8, 16, 8, 1024), F32), pltpu.VMEM((8, 16, 8, 128), F32)],
    )

    slopes, actives, products = [None] * 8, [None] * 8, [None] * 8
    for group in ((0, 1), (2, 6), (3, 7), (4, 5)):
        made = call(
            factors,
            [sds((128, 896))] * (3 * len(group)),
            [pairs[k] for k in group],
            flops=30 * 128 * 896 * len(group),
        )
        for j, k in enumerate(group):
            slopes[k], actives[k], products[k] = made[3 * j : 3 * j + 3]
    down_own, down_other = call(
        partial_down,
        [sds((256, 896), F32), sds((256, 896))],
        (dyw, *products),
        flops=2 * 1024 * 512 * 896,
        scratch=[pltpu.VMEM((1024, 896), BF)],
    )
    down_in = send_core(down_other)

    hids = gather_groups(hid)
    results = []
    for scales in (slopes, actives):
        own, other = call(
            partial_in,
            [sds((256, 896), F32), sds((256, 896))],
            (xw, *scales, *hids),
            flops=2 * 1024 * 512 * 896,
            scratch=[pltpu.VMEM((1024, 896), BF)],
        )
        incoming = send_core(other)
        results.append(own + incoming.astype(F32))
    results.append(down_own + down_in.astype(F32))
    return tuple(results)


def solution(mesh):
    in_specs = (
        P(("dp", "tensor"), None),
        P("dp", "tensor"),
        P("dp", "tensor"),
        P(("dp", "tensor"), None),
        P("dp", "tensor"),
        P(None, "tensor"),
    )
    out_specs = (P("dp", "tensor"), P("dp", "tensor"), P("dp", "tensor"))

    return jax.shard_map(body, mesh=mesh, in_specs=in_specs, out_specs=out_specs, check_vma=False)
```
